256 devices in a mesh: cycle: 16 (over z, core), bin: 16 (over y, x).
Axes of the slice: x: 4, y: 4, z: 8, core: 2. Of those that a mesh axis runs over, the one named last changes fastest.
Arguments:
- obs_minus_bg: bfloat16 [131072, 640], P(('cycle', 'bin')), may hold values from -30 to 30, as said below
- obs_minus_an: bfloat16 [131072, 640], P(('cycle', 'bin')), may hold values from -30 to 30, as said below
- tile_of_row: int32 [131072, 1], P(('cycle', 'bin')), may hold values from 0 to 47; in each aligned block of 512 rows (0 to 511, 512 to 1023, ...) at most 21 rows name the same one
- owner_order: int32 [48], replicated, may hold values from 0 to 47, as said below
Outputs:
- error_cov: float32 [48, 640, 640], P('bin', 'cycle')
The draws below stay inside these ranges and needn't reach their ends.
Inputs may be any that keep to these rules, and one draw needn't show every extreme that they name: `obs_minus_bg`: each row's value lies in this range. `obs_minus_an`: each row's value lies in this range. `tile_of_row`: the rows of one device name one tile at most 21 times; some tile reaches it; every tile is named by some row. `owner_order`: a permutation of the tiles in which entry b * 3 + i is a tile of instrument i, so each index of bin owns one scan bin of each instrument.
All inputs are finite; a program needn't handle non-finite values.
Results may differ from the reference program's by a relative error of at most 0.0003.
Values may be sent and summed in bfloat16 or wider, within the bound.
A program may use at most 320 MiB of HBM per device.

```python
import math
import jax
import jax.numpy as jnp
import numpy as np
from jax import lax

F = 640
C_IASI = 616
C_CRIS = 431
C_ATMS = 22
ROWS_DEV = 512
NTILES = 48
NSCAN = 16
MOSTT = 21
ROWS = 131072
N_CYCLE = 16
N_BIN = 16


def departures(key):
    base = jax.random.fold_in(key, 11)
    key_bias, key_scale, key_noise, key_extra = jax.random.split(base, 4)
    bias = jax.random.uniform(key_bias, (1, F), jnp.float32, -1.0, 1.0)
    scale = jnp.exp(jax.random.uniform(key_scale, (ROWS, 1), jnp.float32, jnp.log(0.5), jnp.log(5.0)))
    noise = jax.random.normal(key_noise, (ROWS, F), jnp.float32)
    first = jnp.clip(bias + scale * noise, -30.0, 30.0)
    second = jnp.clip(0.6 * first + 0.5 * jax.random.normal(key_extra, (ROWS, F), jnp.float32), -30.0, 30.0)
    return (first, second)


def draw_obs_minus_bg(key, part):
    first, second = departures(key)
    return first.astype(jnp.bfloat16)


def draw_obs_minus_an(key, part):
    first, second = departures(key)
    return second.astype(jnp.bfloat16)


def draw_owner_order(key, part):
    base = jax.random.fold_in(key, 23)
    columns = []
    for instrument in range(3):
        shuffled = jax.random.permutation(jax.random.fold_in(base, instrument), NSCAN).astype(jnp.int32)
        columns.append(shuffled + instrument * NSCAN)
    return jnp.stack(columns, axis=1).reshape(-1).astype(jnp.int32)


def deal_out(own_key, own, number, rows, number_of, top, reach, skew):
    order = jax.random.permutation(own_key, number_of)
    packed, ordinary = portions_of(number_of, rows * top, reach, skew, True), portions_of(number_of, rows * top, reach, skew, False)
    places = jnp.arange(number_of)

    def named(tallies, rotation):
        used = int((tallies > 0).sum())
        fixed = max(1, used // 4)
        shifted = fixed + (places - fixed + rotation * (used - fixed)) % max(1, number_of - fixed)
        return jnp.zeros((number_of,), jnp.int32).at[order[jnp.where(places < fixed, places, shifted)]].set(jnp.asarray(tallies, jnp.int32))

    tallies = jnp.where(number % 4 == 0, named(packed, number // 4), named(ordinary, number - number // 4 - 1))
    mixed = jax.random.permutation(jax.random.fold_in(own, 3), number_of)
    giver, taker = mixed[0:number_of // 2 * 2:2], mixed[1:number_of // 2 * 2:2]
    slack = jnp.minimum(tallies[giver] - 1, reach - tallies[taker]) // 2
    slack = jnp.where((giver == order[0]) | (taker == order[0]) | (tallies[taker] == 0), 0, jnp.maximum(slack, 0))
    shifted = jax.random.randint(jax.random.fold_in(own, 4), (number_of // 2,), 0, 1 << 20) % (slack + 1)
    tallies = tallies.at[giver].add(-shifted).at[taker].add(shifted)
    members = jnp.searchsorted(jnp.cumsum(tallies), jnp.arange(rows * top), side="right").astype(jnp.int32)
    table = members.reshape(top, rows).T
    table = table[jax.random.permutation(jax.random.fold_in(own, 1), rows)]
    rotation = jax.random.randint(jax.random.fold_in(own, 2), (rows, 1), 0, top)
    return jnp.take_along_axis(table, (jnp.arange(top)[None, :] + rotation) % top, axis=1)


def portions_of(number_of, total, most, skew, full):
    portions = [(1 << 20) // math.isqrt(rank ** skew) + 1 for rank in range(1, number_of + 1)]
    largest = most if full else min(most, max(-(-total // number_of), total * portions[0] // sum(portions)))
    least = 1 if total - largest >= number_of - 1 else 0
    counts, surplus = [largest] + [least] * (number_of - 1), total - largest - least * (number_of - 1)
    while surplus > 0:
        candidates = [i for i in range(1, number_of) if counts[i] < largest] or [i for i in range(1, number_of) if counts[i] < most]
        whole, left = sum([portions[i] for i in candidates]), surplus
        for i in candidates:
            extra = min(most - counts[i], max(1, left * portions[i] // whole), surplus)
            counts[i] = counts[i] + extra
            surplus = surplus - extra
    return np.array(counts)


def setup_inputs(seed: int = 0) -> dict:
    splits = jax.random.split(jax.random.key(seed), 5)
    obs_minus_bg = draw_obs_minus_bg(jax.random.fold_in(splits[4], 71), 0)
    obs_minus_an = draw_obs_minus_an(jax.random.fold_in(splits[4], 71), 0)
    tile_of_row_keys = jax.random.split(jax.random.fold_in(splits[2], 1), ROWS // ROWS_DEV)
    tile_of_row_turns = jax.random.permutation(jax.random.fold_in(splits[2], 3), ROWS // ROWS_DEV)
    tile_of_row = jax.vmap(lambda own, number: deal_out(jax.random.fold_in(splits[2], 2), own, number, ROWS_DEV, NTILES, 1, MOSTT, 2))(tile_of_row_keys, tile_of_row_turns).reshape((ROWS, 1))
    owner_order = draw_owner_order(jax.random.fold_in(splits[4], 71), 0)
    return dict(obs_minus_bg=obs_minus_bg, obs_minus_an=obs_minus_an, tile_of_row=tile_of_row, owner_order=owner_order)


def reference(obs_minus_bg, obs_minus_an, tile_of_row, owner_order):
    tile = tile_of_row[:, 0]
    instr = tile // NSCAN
    limit = jnp.where(instr == 0, C_IASI, jnp.where(instr == 1, C_CRIS, C_ATMS))
    keep = jnp.arange(F)[None, :] < limit[:, None]
    zero = jnp.zeros((), jnp.bfloat16)
    masked_bg = jnp.where(keep, obs_minus_bg, zero)
    masked_an = jnp.where(keep, obs_minus_an, zero)
    onehot = (tile[:, None] == jnp.arange(NTILES)[None, :]).astype(jnp.int32)
    rank = jnp.sum((jnp.cumsum(onehot, axis=0) - 1) * onehot, axis=1)
    capacity = N_CYCLE * N_BIN * MOSTT
    index_table = jnp.full((NTILES * capacity,), ROWS, jnp.int32)
    index_table = index_table.at[(tile * capacity + rank).astype(jnp.int32)].set(jnp.arange(ROWS, dtype=jnp.int32))
    padded_bg = jnp.concatenate([masked_bg, jnp.zeros((1, F), jnp.bfloat16)], axis=0)
    padded_an = jnp.concatenate([masked_an, jnp.zeros((1, F), jnp.bfloat16)], axis=0)
    count = jnp.sum(onehot, axis=0).astype(jnp.float32)

    def per_tile(t):
        rows_idx = lax.dynamic_slice_in_dim(index_table, (t * capacity).astype(jnp.int32), capacity)
        block_bg = padded_bg[rows_idx]
        block_an = padded_an[rows_idx]
        cross = jnp.dot(block_bg.T, block_an, preferred_element_type=jnp.float32)
        return cross, jnp.sum(block_bg.astype(jnp.float32), axis=0), jnp.sum(block_an.astype(jnp.float32), axis=0)

    cross_sum, sum_bg, sum_an = lax.map(per_tile, jnp.arange(NTILES, dtype=jnp.int32))
    cross_sum = cross_sum[owner_order]
    mean_bg = sum_bg[owner_order] / count[owner_order][:, None]
    mean_an = sum_an[owner_order] / count[owner_order][:, None]
    return cross_sum / count[owner_order][:, None, None] - mean_bg[:, :, None] * mean_an[:, None, :]
```

```python
import jax
import jax.numpy as jnp
from jax import lax
from jax.sharding import PartitionSpec as P

C_IASI = 616
C_CRIS = 431
C_ATMS = 22


def make_moments(width, pieces):
    received, tile_counts = pieces
    part_bg = received[..., :width]
    part_an = received[..., width:]
    cross = jnp.einsum("skrc,skrd->kcd", part_bg, part_an, preferred_element_type=jnp.float32)
    sums = jnp.sum(received, axis=(0, 2), dtype=jnp.float32)
    number = jnp.sum(tile_counts, axis=0).astype(jnp.float32)
    return (cross, sums, number)


def on_device(obs_minus_bg, obs_minus_an, tile_of_row, owner_order):
    n_bin = lax.axis_size("bin")
    n_cycle = lax.axis_size("cycle")
    rows = tile_of_row.shape[0]
    width = obs_minus_bg.shape[1]
    tiles = owner_order.shape[0]
    per_owner = tiles // n_bin
    slot_cap = 2 * rows // tiles
    scan_bins = tiles // 3
    tile = tile_of_row[:, 0]
    instr = tile // scan_bins
    limit = jnp.where(instr == 0, C_IASI, jnp.where(instr == 1, C_CRIS, C_ATMS))
    keep = jnp.arange(width)[None, :] < limit[:, None]
    zero = jnp.zeros((), jnp.bfloat16)
    masked_bg = jnp.where(keep, obs_minus_bg, zero)
    masked_an = jnp.where(keep, obs_minus_an, zero)
    onehot = (tile[:, None] == jnp.arange(tiles)[None, :]).astype(jnp.int32)
    rank = jnp.sum((jnp.cumsum(onehot, axis=0) - 1) * onehot, axis=1)
    order_hits = (owner_order[:, None] == jnp.arange(tiles)[None, :]).astype(jnp.int32)
    position = jnp.sum(order_hits * jnp.arange(tiles, dtype=jnp.int32)[:, None], axis=0)
    row_position = jnp.sum(onehot * position[None, :], axis=1)
    counts = jnp.sum(onehot, axis=0)
    counts_owner = jnp.sum(order_hits * counts[None, :], axis=1).reshape(n_bin, per_owner)
    stacked = jnp.concatenate([masked_bg, masked_an], axis=1)
    dest = row_position * slot_cap + rank
    sendbuf = jnp.zeros((tiles * slot_cap, 2 * width), jnp.bfloat16).at[dest].set(stacked)
    sendbuf = sendbuf.reshape(n_bin, per_owner, slot_cap, 2 * width)
    cross, sums, number = make_moments(
        width,
        (
            lax.all_to_all(sendbuf, "bin", split_axis=0, concat_axis=0, tiled=True),
            lax.all_to_all(counts_owner, "bin", split_axis=0, concat_axis=0, tiled=True),
        ),
    )
    rows_c = width // n_cycle
    start = lax.axis_index("cycle") * rows_c
    cross_rows = lax.psum_scatter(cross, "cycle", scatter_dimension=1, tiled=True)
    sums, number = lax.psum((sums, number), "cycle")
    mean_bg = sums[:, :width] / number[:, None]
    mean_an = sums[:, width:] / number[:, None]
    mean_rows = lax.dynamic_slice_in_dim(mean_bg, start, rows_c, 1)
    return cross_rows / number[:, None, None] - mean_rows[:, :, None] * mean_an[:, None, :]

def solution(mesh):
    return jax.shard_map(
        on_device,
        mesh=mesh,
        in_specs=(
            P(("cycle", "bin"), None),
            P(("cycle", "bin"), None),
            P(("cycle", "bin"), None),
            P(),
        ),
        out_specs=P("bin", "cycle", None),
        check_vma=False,
    )
```
